32 devices in a mesh: tm: 8 (over z, core), row: 4 (over y, x).
Axes of the slice: x: 2, y: 2, z: 4, core: 2. Of those that a mesh axis runs over, the one named last changes fastest.
Arguments:
- element_trans: float32 [8, 512, 512], P('tm', 'row'), may hold values from -1.5 to 1.5
- element_mean: float32 [8, 512], P('tm', 'row'), may hold values from -4 to 4
- element_cov: float32 [8, 512, 512], P('tm', 'row'), may hold values from -2 to 6, as said below
- element_info: float32 [8, 512, 512], P('tm', 'row'), may hold values from -2 to 4, as said below
- element_pull: float32 [8, 512], P('tm', 'row'), may hold values from -4 to 4
- dynamics: float32 [8, 512, 512], P('tm'), may hold values from -0.25 to 0.25
- process_noise: float32 [8, 512, 512], P('tm'), may hold values from -2 to 4, as said below
Outputs:
- smoothed_mean: float32 [8, 512], P('tm', 'row')
- filtered_mean: float32 [8, 512], P('tm', 'row')
- filtered_covariance: float32 [8, 512, 512], P('tm', 'row')
The draws below stay inside these ranges and needn't reach their ends.
Inputs may be any that keep to these rules, and one draw needn't show every extreme that they name: `element_cov`: every step's matrix is symmetric positive definite. `element_info`: every step's matrix is symmetric positive semidefinite. `process_noise`: every step's matrix is symmetric positive definite.
All inputs are finite; a program needn't handle non-finite values.
Results may differ from the reference program's by a relative error of at most 0.0003.
Values sent between devices are 32-bit elements; how exact they have to be, the bound alone decides.
No kernel may reach another device: no remote copies, remote signals or barrier semaphores. Data moves between devices by JAX's collectives and lax.ppermute only.
A program may use at most 128 MiB of HBM per device.

```python
import math
import jax
import jax.numpy as jnp
from jax import lax

OCEAN_VARIABLES = 512
EPOCH_COUNT = 8


def rough_normal(key, shape):
    return jax.random.normal(key, shape, jnp.float32)


def spd_stack(key, floor_value, spread_value):
    sampler_seeds = jax.random.split(key, 2)
    factor_rows = rough_normal(sampler_seeds[0], (EPOCH_COUNT, OCEAN_VARIABLES, OCEAN_VARIABLES))
    scales = jnp.exp(jax.random.uniform(sampler_seeds[1], (EPOCH_COUNT, OCEAN_VARIABLES), jnp.float32, math.log(0.7), math.log(1.4)))
    gram = jnp.einsum('tik,tjk->tij', factor_rows, factor_rows) * (spread_value / OCEAN_VARIABLES)
    based = gram + floor_value * jnp.eye(OCEAN_VARIABLES, dtype=jnp.float32)
    return based * scales[:, :, None] * scales[:, None, :]


def draw_element_cov(key, part):
    return spd_stack(jax.random.fold_in(key, 21), 0.3, 0.5)


def draw_element_info(key, part):
    return spd_stack(jax.random.fold_in(key, 22), 0.0, 0.3)


def draw_process_noise(key, part):
    return spd_stack(jax.random.fold_in(key, 23), 0.2, 0.25)


def draw_element_trans(key, part):
    sampler_seeds = jax.random.split(jax.random.fold_in(key, 31), 4)
    modes_basis = jax.random.orthogonal(sampler_seeds[0], OCEAN_VARIABLES)
    decay_coefficient = jnp.exp(jax.random.uniform(sampler_seeds[1], (EPOCH_COUNT, OCEAN_VARIABLES), jnp.float32, math.log(0.01), math.log(0.6)))
    shock_amplitude = jax.random.uniform(sampler_seeds[2], (EPOCH_COUNT, OCEAN_VARIABLES), jnp.float32) < 0.05
    persistence_coefficient = jnp.where(shock_amplitude, 0.6, 1.0 - decay_coefficient)
    noise_part = rough_normal(sampler_seeds[3], (EPOCH_COUNT, OCEAN_VARIABLES, OCEAN_VARIABLES)) * (0.03 / math.sqrt(OCEAN_VARIABLES))
    return jnp.einsum('ik,tk,jk->tij', modes_basis, persistence_coefficient, modes_basis) + noise_part


def level_of(own_key, shape, pieces, smallest, top_value):
    def one(dim, shards_of):
        steps = jax.random.uniform(jax.random.fold_in(jax.random.fold_in(own_key, 6), dim), (shards_of,), jnp.float32, smallest / len(pieces), top_value / len(pieces))
        return jnp.repeat(jnp.exp(steps), shape[dim] // shards_of).reshape((-1,) + (1,) * (len(shape) - dim - 1))

    loudness = one(*pieces[0])
    for cut in pieces[1:]:
        loudness = loudness * one(*cut)
    return loudness


def noise(key, shape, spread, reach, shards=(), held_as=jnp.bfloat16):
    loudness = level_of(key, shape, shards, -0.22, 0.18) if shards else 1.0
    array = jax.random.normal(key, shape, jnp.float32) * spread * loudness
    return jnp.minimum(jnp.maximum(array, -reach), reach).astype(held_as)


def setup_inputs(seed: int = 0) -> dict:
    keys = jax.random.split(jax.random.key(seed), 8)
    element_trans = draw_element_trans(jax.random.fold_in(keys[7], 71), 0)
    element_mean = noise(keys[1], (EPOCH_COUNT, OCEAN_VARIABLES), 0.5, 4.0, ((0, 8), (1, 4)), jnp.float32)
    element_cov = draw_element_cov(jax.random.fold_in(keys[7], 71), 0)
    element_info = draw_element_info(jax.random.fold_in(keys[7], 71), 0)
    element_pull = noise(keys[4], (EPOCH_COUNT, OCEAN_VARIABLES), 0.5, 4.0, ((0, 8), (1, 4)), jnp.float32)
    dynamics = noise(keys[5], (EPOCH_COUNT, OCEAN_VARIABLES, OCEAN_VARIABLES), OCEAN_VARIABLES ** -0.5, 0.25, ((0, 8),), jnp.float32)
    process_noise = draw_process_noise(jax.random.fold_in(keys[7], 71), 0)
    return {"element_trans": element_trans, "element_mean": element_mean, "element_cov": element_cov, "element_info": element_info, "element_pull": element_pull, "dynamics": dynamics, "process_noise": process_noise}


HIGHEST = lax.Precision.HIGHEST

def multiply_arrays(lhs_mat, rhs_mat):
    return jnp.dot(lhs_mat.astype(jnp.float32), rhs_mat.astype(jnp.float32), precision=HIGHEST, preferred_element_type=jnp.float32)

def spd_solve(lower_factor, rhs_mat):
    middle = lax.linalg.triangular_solve(lower_factor, rhs_mat, left_side=True, lower=True)
    return lax.linalg.triangular_solve(lower_factor, middle, left_side=True, lower=True, transpose_a=True)

def reference(element_trans, element_mean, element_cov, element_info, element_pull, dynamics, process_noise):

    def forward(carried, inputs):
        mean_now, cov_now = carried
        trans_next, mean_next, cov_next, info_next, pull_next = inputs
        stacked = cov_now + multiply_arrays(multiply_arrays(cov_now, info_next), cov_now)
        factor = jnp.linalg.cholesky(stacked)
        leading = multiply_arrays(trans_next, cov_now)
        weighted = multiply_arrays(spd_solve(factor, leading.T).T, cov_now)
        passed = trans_next - multiply_arrays(weighted, info_next)
        mean_new = multiply_arrays(passed, mean_now) + multiply_arrays(weighted, pull_next) + mean_next
        cov_new = multiply_arrays(weighted, trans_next.T) + cov_next
        return ((mean_new, cov_new), (mean_new, cov_new))
    initial = (element_mean[0], element_cov[0])
    _, (means_rest, covs_rest) = lax.scan(forward, initial, (element_trans[1:], element_mean[1:], element_cov[1:], element_info[1:], element_pull[1:]))
    filtered_mean = jnp.concatenate([element_mean[:1], means_rest], axis=0)
    filtered_covariance = jnp.concatenate([element_cov[:1], covs_rest], axis=0)

    def gain_step(inputs):
        propagate_dynamics_once, noise_step, cov_now, mean_now = inputs
        projected = multiply_arrays(propagate_dynamics_once, cov_now)
        innovation = multiply_arrays(projected, propagate_dynamics_once.T) + noise_step
        factor = jnp.linalg.cholesky(innovation)
        gain_mat = spd_solve(factor, projected).T
        offset = mean_now - multiply_arrays(gain_mat, multiply_arrays(propagate_dynamics_once, mean_now))
        return (gain_mat, offset)
    gain_all, offset_all = lax.map(gain_step, (dynamics, process_noise, filtered_covariance, filtered_mean))
    last_index = gain_all.shape[0] - 1

    def backward(carried, inputs):
        gain_mat, offset = inputs
        smoothed_now = multiply_arrays(gain_mat, carried) + offset
        return (smoothed_now, smoothed_now)
    _, smoothed_rest = lax.scan(backward, filtered_mean[last_index], (gain_all[:last_index], offset_all[:last_index]), reverse=True)
    smoothed_mean = jnp.concatenate([smoothed_rest, filtered_mean[last_index:]], axis=0)
    return (smoothed_mean, filtered_mean, filtered_covariance)
```

```python
import functools
import jax, jax.numpy as jnp
from jax import lax
from jax.experimental import pallas as pl
from jax.experimental.pallas import tpu as pltpu
from jax.sharding import PartitionSpec as P

BLOCK, PANEL = 128, 8


def halves(x):
    top = x.astype(jnp.bfloat16)
    return top, (x - top.astype(jnp.float32)).astype(jnp.bfloat16)


def dot3(lhs, rhs, dims):
    lt, ll = lhs
    rt, rl = rhs
    f = lambda a, b: lax.dot_general(a, b, (dims, ((), ())), preferred_element_type=jnp.float32)
    return f(lt, rt) + (f(lt, rl) + f(ll, rt))


def factor_kernel(m_ref, k_ref, work, tiles, inv_d):
    n = m_ref.shape[0]
    count = n // BLOCK
    panels = BLOCK // PANEL
    work[...] = m_ref[...]
    lane = lax.broadcasted_iota(jnp.int32, (PANEL, BLOCK), 1)
    sub = lax.broadcasted_iota(jnp.int32, (PANEL, BLOCK), 0)

    def block_step(b, carry):
        top = pl.multiple_of(b * BLOCK, BLOCK)
        for i in range(count):
            at = pl.multiple_of(lax.rem(b + i, count) * BLOCK, BLOCK)
            tiles[i] = work[pl.ds(top, BLOCK), pl.ds(at, BLOCK)]
        for p in range(panels):
            r0 = PANEL * p
            r1 = r0 + PANEL
            diag = tiles[0, r0:r1, :]
            cols = [jnp.broadcast_to(diag[:, r0 + j : r0 + j + 1], (PANEL, BLOCK)) for j in range(PANEL)]
            here = (lane >= r0) & (lane < r1)
            rows = [jnp.where(here, (lane - r0 == sub).astype(jnp.float32), diag)]
            rows += [tiles[i, r0:r1, :] for i in range(1, count)]
            rec = []
            ups = []
            for j in range(PANEL):
                r = 1.0 / cols[j][j : j + 1, :]
                rec.append(r)
                if j == PANEL - 1:
                    break
                mult = jnp.where(sub > j, cols[j] * r, 0.0)
                up = {}
                for l in range(j + 1, PANEL):
                    up[l] = cols[l][j : j + 1, :]
                    cols[l] = cols[l] - mult * up[l]
                ups.append(up)
                rows = [x - mult * x[j : j + 1, :] for x in rows]
            for i in range(count):
                tiles[i, r0:r1, :] = rows[i]
            inv_d[r0:r1, :] = jnp.concatenate(rec, axis=0)
            for q in range(p + 1, panels):
                s0 = PANEL * q
                s1 = s0 + PANEL
                below = tiles[0, s0:s1, :]
                bc = [jnp.broadcast_to(below[:, r0 + j : r0 + j + 1], (PANEL, BLOCK)) for j in range(PANEL)]
                mults = []
                for j in range(PANEL):
                    m = bc[j] * rec[j]
                    mults.append(m)
                    for l in range(j + 1, PANEL):
                        bc[l] = bc[l] - m * ups[j][l]
                for i in range(count):
                    x = jnp.where(here, 0.0, below) if i == 0 else tiles[i, s0:s1, :]
                    for j in range(PANEL):
                        x = x - mults[j] * rows[i][j : j + 1, :]
                    tiles[i, s0:s1, :] = x
        tri = lax.broadcasted_iota(jnp.int32, (BLOCK, BLOCK), 1) <= lax.broadcasted_iota(jnp.int32, (BLOCK, BLOCK), 0)
        tiles[0] = jnp.where(tri, tiles[0], 0.0)
        scale = lax.rsqrt(inv_d[...])
        scale = inv_d[...] * scale
        for i in range(count):
            at = pl.multiple_of(lax.rem(b + i, count) * BLOCK, BLOCK)
            k_ref[pl.ds(top, BLOCK), pl.ds(at, BLOCK)] = tiles[i] * scale
        kb = k_ref[pl.ds(top, BLOCK), :]
        parts = halves(kb)
        whole_lane = lax.broadcasted_iota(jnp.int32, (BLOCK, n), 1)

        def trail(c, carry):
            low = pl.multiple_of(c * BLOCK, BLOCK)
            lhs = halves(k_ref[pl.ds(top, BLOCK), pl.ds(low, BLOCK)])
            old = work[pl.ds(low, BLOCK), :]
            old = jnp.where((whole_lane >= top) & (whole_lane < top + BLOCK), 0.0, old)
            work[pl.ds(low, BLOCK), :] = old - dot3(lhs, parts, ((0,), (0,)))
            return carry

        lax.fori_loop(b + 1, count, trail, 0)
        k_ref[pl.ds(top, BLOCK), :] = jnp.where(whole_lane < top + BLOCK, kb, 0.0)
        return carry

    lax.fori_loop(0, count, block_step, 0)


def factor(m):
    n = m.shape[0]
    return pl.pallas_call(
        factor_kernel,
        out_shape=jax.ShapeDtypeStruct((n, n), jnp.float32),
        in_specs=[pl.BlockSpec(memory_space=pltpu.VMEM)],
        out_specs=pl.BlockSpec(memory_space=pltpu.VMEM),
        scratch_shapes=[
            pltpu.VMEM((n, n), jnp.float32),
            pltpu.VMEM((n // BLOCK, BLOCK, BLOCK), jnp.float32),
            pltpu.VMEM((BLOCK, BLOCK), jnp.float32),
        ],
        cost_estimate=pl.CostEstimate(flops=40 * n**3, bytes_accessed=8 * n * n, transcendentals=0),
        name="factor",
    )(m)


def shifted(block, axis, distance):
    devices = range(lax.axis_size(axis))
    route = [(i - distance, i) for i in devices if i - distance in devices]
    return lax.ppermute(block, axis, route)


def product(lhs, rhs, dims=((1,), (0,))):
    return lax.dot_general(
        lhs, rhs, (dims, ((), ())), precision=lax.Precision.HIGH, preferred_element_type=jnp.float32
    )


def apply(mat, vec):
    return jnp.sum(mat * vec[None, :], axis=1)


def apply_t(mat, vec):
    return jnp.sum(mat * vec[:, None], axis=0)


NT = ((1,), (1,))
TN = ((0,), (0,))


def gather_rows(rows):
    return lax.all_gather(rows, "row", axis=0, tiled=True)


def body(element_trans, element_mean, element_cov, element_info, element_pull, dynamics, process_noise):
    time_pos = lax.axis_index("tm")
    row_pos = lax.axis_index("row")
    time_count = lax.axis_size("tm")
    row_count, n = element_trans.shape[1:]
    mine = lambda whole: lax.dynamic_slice_in_dim(whole, row_pos * row_count, row_count, 0)
    keep = jnp.where(time_pos == 0, 0.0, 1.0)
    eye = jnp.eye(n, dtype=jnp.float32)
    cov_rows = element_cov[0]
    info = gather_rows(element_info[0] * keep)
    vectors = jnp.concatenate([element_mean[0], element_pull[0] * keep])
    extra = jnp.pad(vectors[None], ((0, 7), (0, n - 2 * row_count)))
    packed = lax.all_gather(jnp.concatenate([element_trans[0] * keep, extra]), "row", axis=0)
    trans = packed[:, :row_count].reshape(n, n)
    mean = packed[:, row_count, :row_count].reshape(n)
    pull = packed[:, row_count, row_count : 2 * row_count].reshape(n)
    levels = (time_count - 1).bit_length()
    for level in range(levels):
        distance = 1 << level
        closing = level == levels - 1
        absent = jnp.where(time_pos >= distance, 0.0, 1.0)
        cov1 = gather_rows(shifted(cov_rows, "tm", distance))
        if closing:
            cov = gather_rows(cov_rows)
            mean1 = shifted(mean, "tm", distance)
        else:
            rows1 = shifted(jnp.concatenate([mine(trans), mine(info)]), "tm", distance)
            both = lax.all_gather(rows1, "row", axis=0)
            trans1 = both[:, :row_count].reshape(n, n) + absent * eye
            info1 = both[:, row_count:].reshape(n, n)
            mean1, pull1 = shifted(jnp.stack([mean, pull]), "tm", distance)
        mixed = cov1 + product(cov1, product(info, cov1)) + absent * eye
        root = factor(mixed)
        right = product(product(trans, cov1), root, NT)
        left = product(root, cov1)
        rest = pull - apply(info, mean1)
        inner = apply(left, rest)
        mean_new = apply(trans, mean1) + apply(right, inner) + mean
        if closing:
            cov = cov + product(right, right, NT)
            mean = mean_new
            break
        cov_rows = cov_rows + product(mine(right), right, NT)
        turned = product(info, trans1)
        bridge = product(left, turned)
        pull = apply_t(trans1, rest) - apply_t(bridge, inner) + pull1
        info = product(trans1, turned, TN) - product(bridge, bridge, TN) + info1
        trans = product(trans, trans1) - product(right, bridge)
        mean = mean_new
    step = dynamics[0]
    projected = product(step, cov)
    root = factor(product(projected, step, NT) + process_noise[0])
    gain = product(product(root, projected), root, TN)
    offset = mean - apply(gain, apply(step, mean))
    smoothed = mean
    for back in range(time_count - 2, -1, -1):
        later = shifted(smoothed, "tm", -1)
        smoothed = jnp.where(time_pos == back, apply(gain, later) + offset, smoothed)
    return (mine(smoothed)[None], mine(mean)[None], mine(cov)[None])


def solution(mesh):
    rows, vecs, whole = P("tm", "row", None), P("tm", "row"), P("tm", None, None)
    return jax.shard_map(
        body,
        mesh=mesh,
        in_specs=(rows, vecs, rows, rows, vecs, whole, whole),
        out_specs=(vecs, vecs, rows),
        check_vma=False,
    )
```

```python
import functools
import jax, jax.numpy as jnp
from jax import lax
from jax.experimental import pallas as pl
from jax.experimental.pallas import tpu as pltpu
from jax.sharding import PartitionSpec as P

BLOCK, PANEL = 128, 8


def halves(x):
    top = x.astype(jnp.bfloat16)
    return top, (x - top.astype(jnp.float32)).astype(jnp.bfloat16)


def dot3(lhs, rhs, dims):
    lt, ll = lhs
    rt, rl = rhs
    f = lambda a, b: lax.dot_general(a, b, (dims, ((), ())), preferred_element_type=jnp.float32)
    return f(lt, rt) + (f(lt, rl) + f(ll, rt))


def factor_kernel(m_ref, k_ref, work, tiles, inv_d):
    n = m_ref.shape[0]
    count = n // BLOCK
    panels = BLOCK // PANEL
    work[...] = m_ref[...]
    lane = lax.broadcasted_iota(jnp.int32, (PANEL, BLOCK), 1)
    sub = lax.broadcasted_iota(jnp.int32, (PANEL, BLOCK), 0)

    def block_step(b, carry):
        top = pl.multiple_of(b * BLOCK, BLOCK)
        for i in range(count):
            at = pl.multiple_of(lax.rem(b + i, count) * BLOCK, BLOCK)
            tiles[i] = work[pl.ds(top, BLOCK), pl.ds(at, BLOCK)]
        for p in range(panels):
            r0 = PANEL * p
            r1 = r0 + PANEL
            diag = tiles[0, r0:r1, :]
            cols = [jnp.broadcast_to(diag[:, r0 + j : r0 + j + 1], (PANEL, BLOCK)) for j in range(PANEL)]
            here = (lane >= r0) & (lane < r1)
            rows = [jnp.where(here, (lane - r0 == sub).astype(jnp.float32), diag)]
            rows += [tiles[i, r0:r1, :] for i in range(1, count)]
            rec = []
            ups = []
            for j in range(PANEL):
                r = 1.0 / cols[j][j : j + 1, :]
                rec.append(r)
                if j == PANEL - 1:
                    break
                mult = jnp.where(sub > j, cols[j] * r, 0.0)
                up = {}
                for l in range(j + 1, PANEL):
                    up[l] = cols[l][j : j + 1, :]
                    cols[l] = cols[l] - mult * up[l]
                ups.append(up)
                rows = [x - mult * x[j : j + 1, :] for x in rows]
            for i in range(count):
                tiles[i, r0:r1, :] = rows[i]
            inv_d[r0:r1, :] = jnp.concatenate(rec, axis=0)
            for q in range(p + 1, panels):
                s0 = PANEL * q
                s1 = s0 + PANEL
                below = tiles[0, s0:s1, :]
                bc = [jnp.broadcast_to(below[:, r0 + j : r0 + j + 1], (PANEL, BLOCK)) for j in range(PANEL)]
                mults = []
                for j in range(PANEL):
                    m = bc[j] * rec[j]
                    mults.append(m)
                    for l in range(j + 1, PANEL):
                        bc[l] = bc[l] - m * ups[j][l]
                for i in range(count):
                    x = jnp.where(here, 0.0, below) if i == 0 else tiles[i, s0:s1, :]
                    for j in range(PANEL):
                        x = x - mults[j] * rows[i][j : j + 1, :]
                    tiles[i, s0:s1, :] = x
        tri = lax.broadcasted_iota(jnp.int32, (BLOCK, BLOCK), 1) <= lax.broadcasted_iota(jnp.int32, (BLOCK, BLOCK), 0)
        tiles[0] = jnp.where(tri, tiles[0], 0.0)
        scale = lax.rsqrt(inv_d[...])
        scale = inv_d[...] * scale
        for i in range(count):
            at = pl.multiple_of(lax.rem(b + i, count) * BLOCK, BLOCK)
            k_ref[pl.ds(top, BLOCK), pl.ds(at, BLOCK)] = tiles[i] * scale
        kb = k_ref[pl.ds(top, BLOCK), :]
        parts = halves(kb)
        whole_lane = lax.broadcasted_iota(jnp.int32, (BLOCK, n), 1)

        def trail(c, carry):
            low = pl.multiple_of(c * BLOCK, BLOCK)
            lhs = halves(k_ref[pl.ds(top, BLOCK), pl.ds(low, BLOCK)])
            old = work[pl.ds(low, BLOCK), :]
            old = jnp.where((whole_lane >= top) & (whole_lane < top + BLOCK), 0.0, old)
            work[pl.ds(low, BLOCK), :] = old - dot3(lhs, parts, ((0,), (0,)))
            return carry

        lax.fori_loop(b + 1, count, trail, 0)
        k_ref[pl.ds(top, BLOCK), :] = jnp.where(whole_lane < top + BLOCK, kb, 0.0)
        return carry

    lax.fori_loop(0, count, block_step, 0)


def factor(m):
    n = m.shape[0]
    return pl.pallas_call(
        factor_kernel,
        out_shape=jax.ShapeDtypeStruct((n, n), jnp.float32),
        in_specs=[pl.BlockSpec(memory_space=pltpu.VMEM)],
        out_specs=pl.BlockSpec(memory_space=pltpu.VMEM),
        scratch_shapes=[
            pltpu.VMEM((n, n), jnp.float32),
            pltpu.VMEM((n // BLOCK, BLOCK, BLOCK), jnp.float32),
            pltpu.VMEM((BLOCK, BLOCK), jnp.float32),
        ],
        cost_estimate=pl.CostEstimate(flops=40 * n**3, bytes_accessed=8 * n * n, transcendentals=0),
        name="factor",
    )(m)


def shifted(block, axis, distance):
    devices = range(lax.axis_size(axis))
    route = [(i - distance, i) for i in devices if i - distance in devices]
    return lax.ppermute(block, axis, route)


def product(lhs, rhs, dims=((1,), (0,))):
    return lax.dot_general(
        lhs, rhs, (dims, ((), ())), precision=lax.Precision.HIGH, preferred_element_type=jnp.float32
    )


def apply(mat, vec):
    return jnp.sum(mat * vec[None, :], axis=1)


def apply_t(mat, vec):
    return jnp.sum(mat * vec[:, None], axis=0)


NT = ((1,), (1,))
TN = ((0,), (0,))


def from_peers(block):
    peers = range(lax.axis_size("row"))
    return [block] + [lax.ppermute(block, "row", [(i, i ^ k) for i in peers]) for k in peers if k]


def gather(block):
    row_pos = lax.axis_index("row")
    pieces = from_peers(block)
    whole = jnp.zeros((len(pieces),) + block.shape, block.dtype)
    for k, piece in enumerate(pieces):
        whole = lax.dynamic_update_slice(whole, piece[None], (row_pos ^ k,) + (0,) * block.ndim)
    return whole


def body(element_trans, element_mean, element_cov, element_info, element_pull, dynamics, process_noise):
    time_pos = lax.axis_index("tm")
    row_pos = lax.axis_index("row")
    time_count = lax.axis_size("tm")
    row_count, n = element_trans.shape[1:]
    mine = lambda whole: lax.dynamic_slice_in_dim(whole, row_pos * row_count, row_count, 0)
    keep = jnp.where(time_pos == 0, 0.0, 1.0)
    eye = jnp.eye(n, dtype=jnp.float32)
    cov_rows = element_cov[0]
    info_rows = element_info[0] * keep
    trans_rows = element_trans[0] * keep
    info = gather(info_rows).reshape(n, n)
    vectors = jnp.concatenate([element_mean[0], element_pull[0] * keep])
    extra = jnp.pad(vectors[None], ((0, 7), (0, n - 2 * row_count)))
    levels = (time_count - 1).bit_length()
    for level in range(levels):
        distance = 1 << level
        closing = level == levels - 1
        absent = jnp.where(time_pos >= distance, 0.0, 1.0)
        cov1 = gather(shifted(cov_rows, "tm", distance)).reshape(n, n)
        if level == 0:
            cov1, trans_rows, extra = lax.optimization_barrier((cov1, trans_rows, extra))
            packed = gather(jnp.concatenate([trans_rows, extra]))
            trans = packed[:, :row_count].reshape(n, n)
            mean = packed[:, row_count, :row_count].reshape(n)
            pull = packed[:, row_count, row_count : 2 * row_count].reshape(n)
        if closing:
            cov = gather(cov_rows).reshape(n, n)
            mean1 = shifted(mean, "tm", distance)
        else:
            rows1 = shifted(jnp.concatenate([trans_rows, info_rows]), "tm", distance)
            both = gather(rows1)
            trans1 = both[:, :row_count].reshape(n, n) + absent * eye
            info1 = both[:, row_count:].reshape(n, n)
            mean1, pull1 = shifted(jnp.stack([mean, pull]), "tm", distance)
        mixed = cov1 + product(cov1, product(info, cov1)) + absent * eye
        root = factor(mixed)
        right = product(product(trans, cov1), root, NT)
        left = product(root, cov1)
        rest = pull - apply(info, mean1)
        inner = apply(left, rest)
        mean_new = apply(trans, mean1) + apply(right, inner) + mean
        if closing:
            cov = cov + product(right, right, NT)
            mean = mean_new
            break
        cov_rows = cov_rows + product(mine(right), right, NT)
        turned = product(info, trans1)
        bridge = product(left, turned)
        pull = apply_t(trans1, rest) - apply_t(bridge, inner) + pull1
        info = product(trans1, turned, TN) - product(bridge, bridge, TN) + info1
        trans = product(trans, trans1) - product(right, bridge)
        trans_rows, info_rows = mine(trans), mine(info)
        mean = mean_new
    step = dynamics[0]
    projected = product(step, cov)
    root = factor(product(projected, step, NT) + process_noise[0])
    gain = product(product(root, projected), root, TN)
    offset = mean - apply(gain, apply(step, mean))
    smoothed = mean
    for back in range(time_count - 2, -1, -1):
        later = lax.ppermute(smoothed, "tm", [(back + 1, back)])
        smoothed = jnp.where(time_pos == back, apply(gain, later) + offset, smoothed)
    return (mine(smoothed)[None], mine(mean)[None], mine(cov)[None])


def solution(mesh):
    rows, vecs, whole = P("tm", "row", None), P("tm", "row"), P("tm", None, None)
    return jax.shard_map(
        body,
        mesh=mesh,
        in_specs=(rows, vecs, rows, rows, vecs, whole, whole),
        out_specs=(vecs, vecs, rows),
        check_vma=False,
    )
```

```python
import functools
import jax, jax.numpy as jnp
from jax import lax
from jax.experimental import pallas as pl
from jax.experimental.pallas import tpu as pltpu
from jax.sharding import PartitionSpec as P

BLOCK, PANEL = 128, 8


def halves(x):
    top = x.astype(jnp.bfloat16)
    return top, (x - top.astype(jnp.float32)).astype(jnp.bfloat16)


def dot3(lhs, rhs, dims):
    lt, ll = lhs
    rt, rl = rhs
    f = lambda a, b: lax.dot_general(a, b, (dims, ((), ())), preferred_element_type=jnp.float32)
    return f(lt, rt) + (f(lt, rl) + f(ll, rt))


def eliminate(k_ref, work, tiles, inv_d):
    n = work.shape[0]
    count = n // BLOCK
    panels = BLOCK // PANEL
    lane = lax.broadcasted_iota(jnp.int32, (PANEL, BLOCK), 1)
    sub = lax.broadcasted_iota(jnp.int32, (PANEL, BLOCK), 0)

    def block_step(b, carry):
        top = pl.multiple_of(b * BLOCK, BLOCK)
        for i in range(count):
            at = pl.multiple_of(lax.rem(b + i, count) * BLOCK, BLOCK)
            tiles[i] = work[pl.ds(top, BLOCK), pl.ds(at, BLOCK)]
        for p in range(panels):
            r0 = PANEL * p
            r1 = r0 + PANEL
            diag = tiles[0, r0:r1, :]
            cols = [jnp.broadcast_to(diag[:, r0 + j : r0 + j + 1], (PANEL, BLOCK)) for j in range(PANEL)]
            here = (lane >= r0) & (lane < r1)
            rows = [jnp.where(here, (lane - r0 == sub).astype(jnp.float32), diag)]
            rows += [tiles[i, r0:r1, :] for i in range(1, count)]
            rec = []
            ups = []
            for j in range(PANEL):
                r = 1.0 / cols[j][j : j + 1, :]
                rec.append(r)
                if j == PANEL - 1:
                    break
                mult = jnp.where(sub > j, cols[j] * r, 0.0)
                up = {}
                for l in range(j + 1, PANEL):
                    up[l] = cols[l][j : j + 1, :]
                    cols[l] = cols[l] - mult * up[l]
                ups.append(up)
                rows = [x - mult * x[j : j + 1, :] for x in rows]
            for i in range(count):
                tiles[i, r0:r1, :] = rows[i]
            inv_d[r0:r1, :] = jnp.concatenate(rec, axis=0)
            for q in range(p + 1, panels):
                s0 = PANEL * q
                s1 = s0 + PANEL
                below = tiles[0, s0:s1, :]
                bc = [jnp.broadcast_to(below[:, r0 + j : r0 + j + 1], (PANEL, BLOCK)) for j in range(PANEL)]
                mults = []
                for j in range(PANEL):
                    m = bc[j] * rec[j]
                    mults.append(m)
                    for l in range(j + 1, PANEL):
                        bc[l] = bc[l] - m * ups[j][l]
                for i in range(count):
                    x = jnp.where(here, 0.0, below) if i == 0 else tiles[i, s0:s1, :]
                    for j in range(PANEL):
                        x = x - mults[j] * rows[i][j : j + 1, :]
                    tiles[i, s0:s1, :] = x
        tri = lax.broadcasted_iota(jnp.int32, (BLOCK, BLOCK), 1) <= lax.broadcasted_iota(jnp.int32, (BLOCK, BLOCK), 0)
        tiles[0] = jnp.where(tri, tiles[0], 0.0)
        scale = lax.rsqrt(inv_d[...])
        scale = inv_d[...] * scale
        for i in range(count):
            at = pl.multiple_of(lax.rem(b + i, count) * BLOCK, BLOCK)
            k_ref[pl.ds(top, BLOCK), pl.ds(at, BLOCK)] = tiles[i] * scale
        kb = k_ref[pl.ds(top, BLOCK), :]
        parts = halves(kb)
        whole_lane = lax.broadcasted_iota(jnp.int32, (BLOCK, n), 1)

        def trail(c, carry):
            low = pl.multiple_of(c * BLOCK, BLOCK)
            lhs = halves(k_ref[pl.ds(top, BLOCK), pl.ds(low, BLOCK)])
            old = work[pl.ds(low, BLOCK), :]
            old = jnp.where((whole_lane >= top) & (whole_lane < top + BLOCK), 0.0, old)
            work[pl.ds(low, BLOCK), :] = old - dot3(lhs, parts, ((0,), (0,)))
            return carry

        lax.fori_loop(b + 1, count, trail, 0)
        k_ref[pl.ds(top, BLOCK), :] = jnp.where(whole_lane < top + BLOCK, kb, 0.0)
        return carry

    lax.fori_loop(0, count, block_step, 0)


def each_block(n, step):
    def at(i, carry):
        step(pl.ds(pl.multiple_of(i * BLOCK, BLOCK), BLOCK), i)
        return carry

    lax.fori_loop(0, n // BLOCK, at, 0)


def front_kernel(peers, info_peers, pos_ref, absent_ref, *refs):
    cov_pieces, info_pieces = refs[:peers], refs[peers : peers + info_peers]
    outs = refs[peers + info_peers :]
    if info_peers > 1:
        k_ref, c_ref, j_ref = outs[:3]
        outs = outs[3:]
    else:
        k_ref, c_ref = outs[:2]
        j_ref = info_pieces[0]
        outs = outs[2:]
    c_top, c_low, t_top, t_low, work, tiles, inv_d = outs
    n = c_ref.shape[0]
    rows = n // peers
    for k in range(peers):
        at = pl.ds(pl.multiple_of(lax.bitwise_xor(pos_ref[0], k) * rows, rows), rows)
        c_ref[at, :] = cov_pieces[k][...]
        top, low = halves(cov_pieces[k][...])
        c_top[at, :], c_low[at, :] = top, low
        if info_peers > 1:
            j_ref[at, :] = info_pieces[k][...]

    def first(at, i):
        part = dot3(halves(j_ref[at, :]), (c_top[...], c_low[...]), ((1,), (0,)))
        t_top[at, :], t_low[at, :] = halves(part)

    def second(at, i):
        part = dot3((c_top[at, :], c_low[at, :]), (t_top[...], t_low[...]), ((1,), (0,)))
        across = lax.broadcasted_iota(jnp.int32, (BLOCK, n), 1)
        down = lax.broadcasted_iota(jnp.int32, (BLOCK, n), 0) + i * BLOCK
        work[at, :] = c_ref[at, :] + part + jnp.where(across == down, absent_ref[0], 0.0)

    each_block(n, first)
    each_block(n, second)
    eliminate(k_ref, work, tiles, inv_d)


def factor_scratch(n):
    return [
        pltpu.VMEM((n, n), jnp.float32),
        pltpu.VMEM((n // BLOCK, BLOCK, BLOCK), jnp.float32),
        pltpu.VMEM((BLOCK, BLOCK), jnp.float32),
    ]


COST = 20 * 10**9


def front(cov_pieces, info_pieces, row_pos, absent):
    n = cov_pieces[0].shape[1]
    full = jax.ShapeDtypeStruct((n, n), jnp.float32)
    vmem, smem = pl.BlockSpec(memory_space=pltpu.VMEM), pl.BlockSpec(memory_space=pltpu.SMEM)
    outs = 3 if len(info_pieces) > 1 else 2
    return pl.pallas_call(
        functools.partial(front_kernel, len(cov_pieces), len(info_pieces)),
        out_shape=[full] * outs,
        in_specs=[smem, smem] + [vmem] * (len(cov_pieces) + len(info_pieces)),
        out_specs=[vmem] * outs,
        scratch_shapes=[pltpu.VMEM((n, n), jnp.bfloat16)] * 4 + factor_scratch(n),
        cost_estimate=pl.CostEstimate(flops=COST, bytes_accessed=20 * n * n, transcendentals=0),
        name="front",
    )(row_pos.reshape(1), absent.reshape(1), *cov_pieces, *info_pieces)


def factor_kernel(m_ref, k_ref, work, tiles, inv_d):
    work[...] = m_ref[...]
    eliminate(k_ref, work, tiles, inv_d)


def factor(m):
    n = m.shape[0]
    return pl.pallas_call(
        factor_kernel,
        out_shape=jax.ShapeDtypeStruct((n, n), jnp.float32),
        in_specs=[pl.BlockSpec(memory_space=pltpu.VMEM)],
        out_specs=pl.BlockSpec(memory_space=pltpu.VMEM),
        scratch_shapes=factor_scratch(n),
        cost_estimate=pl.CostEstimate(flops=COST, bytes_accessed=8 * n * n, transcendentals=0),
        name="factor",
    )(m)


def shifted(block, axis, distance):
    devices = range(lax.axis_size(axis))
    route = [(i - distance, i) for i in devices if i - distance in devices]
    return lax.ppermute(block, axis, route)


def product(lhs, rhs, dims=((1,), (0,))):
    return lax.dot_general(
        lhs, rhs, (dims, ((), ())), precision=lax.Precision.HIGH, preferred_element_type=jnp.float32
    )


def apply(mat, vec):
    return jnp.sum(mat * vec[None, :], axis=1)


def apply_t(mat, vec):
    return jnp.sum(mat * vec[:, None], axis=0)


NT = ((1,), (1,))
TN = ((0,), (0,))


def from_peers(block):
    peers = range(lax.axis_size("row"))
    return [block] + [lax.ppermute(block, "row", [(i, i ^ k) for i in peers]) for k in peers if k]


def in_order(pieces):
    row_pos = lax.axis_index("row")
    whole = jnp.zeros((len(pieces),) + pieces[0].shape, jnp.float32)
    for k, piece in enumerate(pieces):
        whole = lax.dynamic_update_slice(whole, piece[None], (row_pos ^ k,) + (0,) * piece.ndim)
    return whole


def body(element_trans, element_mean, element_cov, element_info, element_pull, dynamics, process_noise):
    time_pos = lax.axis_index("tm")
    row_pos = lax.axis_index("row")
    time_count = lax.axis_size("tm")
    rows, n = element_trans.shape[1:]
    mine = lambda whole: lax.dynamic_slice_in_dim(whole, row_pos * rows, rows, 0)
    keep = jnp.where(time_pos == 0, 0.0, 1.0)
    eye = jnp.eye(n, dtype=jnp.float32)
    cov_rows = element_cov[0]
    info_rows = element_info[0] * keep
    trans_rows = element_trans[0] * keep
    vectors = jnp.concatenate([element_mean[0], element_pull[0] * keep])
    extra = jnp.pad(vectors[None], ((0, 7), (0, n - 2 * rows)))
    levels = (time_count - 1).bit_length()
    for level in range(levels):
        distance = 1 << level
        opening, closing = level == 0, level == levels - 1
        absent = jnp.where(time_pos >= distance, 0.0, 1.0)
        cov1_rows = shifted(cov_rows, "tm", distance)
        if opening:
            info_pieces = from_peers(info_rows)
        else:
            info_pieces = [info]
        cov1_pieces = from_peers(cov1_rows)
        if closing:
            mean1 = shifted(mean, "tm", distance)
            rest_pieces = from_peers(cov_rows)
        else:
            rest1 = shifted(jnp.concatenate([trans_rows, info_rows, extra]), "tm", distance)
            if opening:
                rest1 = jnp.concatenate([rest1, trans_rows, extra])
            rest_pieces = from_peers(rest1)
        made = front(cov1_pieces, info_pieces, row_pos, absent)
        root, cov1 = made[:2]
        if opening:
            info = made[2]
        packed = in_order(rest_pieces)
        if closing:
            cov = packed.reshape(n, n)
        else:
            trans1 = packed[:, :rows].reshape(n, n) + absent * eye
            info1 = packed[:, rows : 2 * rows].reshape(n, n)
            edge = 2 * rows
            if opening:
                mean1 = packed[:, edge, :rows].reshape(n)
                pull1 = packed[:, edge, rows : 2 * rows].reshape(n)
                edge += 8
                trans = packed[:, edge : edge + rows].reshape(n, n)
                edge += rows
                mean = packed[:, edge, :rows].reshape(n)
                pull = packed[:, edge, rows : 2 * rows].reshape(n)
            else:
                mean1, pull1 = rest1[edge], rest1[edge + 1]
        right = product(product(trans, cov1), root, NT)
        if not closing:
            cov_rows = cov_rows + product(mine(right), right, NT)
        rest = pull - apply(info, mean1)
        inner = apply(root, apply(cov1, rest))
        mean_new = apply(trans, mean1) + apply(right, inner) + mean
        if closing:
            cov = cov + product(right, right, NT)
            mean = mean_new
            break
        turned = product(info, trans1)
        left = product(root, cov1)
        bridge = product(left, turned)
        pull = apply_t(trans1, rest) - apply_t(bridge, inner) + pull1
        info = product(trans1, turned, TN) - product(bridge, bridge, TN) + info1
        trans = product(trans, trans1) - product(right, bridge)
        trans_rows, info_rows = mine(trans), mine(info)
        mean = mean_new
        extra = jnp.pad(jnp.stack([mean, pull]), ((0, 6), (0, 0)))
    step = dynamics[0]
    projected = product(step, cov)
    root = factor(product(projected, step, NT) + process_noise[0])
    gain = product(product(root, projected), root, TN)
    offset = mean - apply(gain, apply(step, mean))
    smoothed = mean
    for back in range(time_count - 2, -1, -1):
        later = lax.ppermute(smoothed, "tm", [(back + 1, back)])
        smoothed = jnp.where(time_pos == back, apply(gain, later) + offset, smoothed)
    return (mine(smoothed)[None], mine(mean)[None], mine(cov)[None])


def solution(mesh):
    rows, vecs, whole = P("tm", "row", None), P("tm", "row"), P("tm", None, None)
    return jax.shard_map(
        body,
        mesh=mesh,
        in_specs=(rows, vecs, rows, rows, vecs, whole, whole),
        out_specs=(vecs, vecs, rows),
        check_vma=False,
    )
```
